32 devices in a mesh: layer: 2 (over core), latent: 8 (over z, x), token: 2 (over y).
Axes of the slice: x: 2, y: 2, z: 4, core: 2. Of those that a mesh axis runs over, the one named last changes fastest.
Arguments:
- taps: bfloat16 [2, 448, 3584], P('layer', 'token'), may hold values from -6 to 6
- token_ids: int32 [448], P('token'), may hold values from 2 to 255999, as said below
- enc_weight: bfloat16 [2, 3584, 2048], P('layer', 'token', 'latent'), may hold values from -0.0625 to 0.0625
- enc_bias: float32 [2048], P('latent'), may hold values from -3 to 3
- dec_weight: bfloat16 [2, 3584, 2048], P('layer', 'token', 'latent'), as said below
- dec_bias: float32 [2, 3584], P('layer'), may hold values from -3 to 3
Outputs:
- enc_grad: bfloat16 [2, 3584, 2048], P('layer', 'token', 'latent')
- dec_grad: bfloat16 [2, 3584, 2048], P('layer', 'token', 'latent')
The draws below stay inside these ranges and needn't reach their ends.
Inputs may be any that keep to these rules, and one draw needn't show every extreme that they name: `token_ids`: id 2 marks the beginning of a document and stands at position 0; all other ids are 3 or more. `dec_weight`: entries of order 2048^-0.5.
All inputs are finite; a program needn't handle non-finite values.
Results may differ from the reference program's by a relative error of at most 0.014.
Values may be sent and summed in bfloat16 or wider, within the bound.
No kernel may reach another device: no remote copies, remote signals or barrier semaphores. Data moves between devices by JAX's collectives and lax.ppermute only.
A program may use at most 64 MiB of HBM per device.

```python
import math
import jax
import jax.numpy as jnp
from jax import lax

D = 3584
VOCAB = 256000
TOK_DEV = 224
LATENTS = 2048
LAYERS = 2
TOKENS = 448
N_TOKEN = 2


def draw_token_ids(key, part):
    folded = jax.random.fold_in(key, 11)
    word_key, begin_key = jax.random.split(folded)
    vocab_ids = jax.random.randint(word_key, (TOKENS,), 3, VOCAB, dtype=jnp.int32)
    starts = jax.random.randint(begin_key, (TOKENS,), 0, 16, dtype=jnp.int32) == 0
    position = jnp.arange(TOKENS, dtype=jnp.int32)
    starts = jnp.logical_or(starts, position == 0)
    return jnp.where(starts, 2, vocab_ids).astype(jnp.int32)


def draw_dec_weight(key, part):
    folded = jax.random.fold_in(key, 23)
    entry_key, row_key, col_key = jax.random.split(folded, 3)
    entries = jax.random.truncated_normal(entry_key, -6.0, 6.0, (LAYERS, D, LATENTS), jnp.float32)
    lower = 0.32
    upper = 3.2
    row_scale = jnp.exp(jax.random.uniform(row_key, (LAYERS, D, 1), jnp.float32, math.log(lower), math.log(upper)))
    col_scale = jnp.exp(jax.random.uniform(col_key, (LAYERS, 1, LATENTS), jnp.float32, math.log(lower), math.log(upper)))
    return (entries * row_scale * col_scale / math.sqrt(5.0 * LATENTS)).astype(jnp.bfloat16)


def block_levels(key, shape, pieces, smallest, largest):
    level, own = 1.0, jax.random.fold_in(key, 6)
    for dim, blocks in pieces:
        steps = jnp.exp(jax.random.uniform(jax.random.fold_in(own, dim), (blocks,), jnp.float32, smallest / len(pieces), largest / len(pieces)))
        level = level * jnp.repeat(steps, shape[dim] // blocks).reshape([-1 if axis == dim else 1 for axis in range(len(shape))])
    return level


def normal_values(own_key, dims, deviation, reach, cuts=(), held_as=jnp.bfloat16):
    result = jax.random.normal(own_key, dims, jnp.float32) * deviation
    if len(cuts) > 0:
        result = block_levels(own_key, dims, cuts, -0.22, 0.18) * result
    return jnp.clip(result, min=-reach, max=reach).astype(held_as)


def setup_inputs(seed: int = 0) -> dict:
    keys = jax.random.split(jax.random.key(seed), 7)
    return {
        "taps": normal_values(keys[0], (LAYERS, TOKENS, D), 1.0, 6.0, ((0, 2), (1, 2))),
        "token_ids": draw_token_ids(jax.random.fold_in(keys[6], 71), 0),
        "enc_weight": normal_values(keys[2], (LAYERS, D, LATENTS), (LAYERS * D) ** -0.5, 0.0625, ((0, 2), (1, 2), (2, 8))),
        "enc_bias": normal_values(keys[3], (LATENTS,), 0.5, 3.0, ((0, 8),), jnp.float32),
        "dec_weight": draw_dec_weight(jax.random.fold_in(keys[6], 71), 0),
        "dec_bias": normal_values(keys[5], (LAYERS, D), 0.5, 3.0, ((0, 2),), jnp.float32),
    }


KNEE_WIDTH = 0.5
SPARSITY = 0.5
BEGIN_TOKEN = 2

def smooth_relu(preact):
    positive = jnp.maximum(preact, 0.0)
    return jnp.where(positive < KNEE_WIDTH, positive * positive / (2.0 * KNEE_WIDTH), positive - 0.5 * KNEE_WIDTH)

def relu_slope(preact):
    return jnp.clip(preact / KNEE_WIDTH, 0.0, 1.0)

def reference(taps, token_ids, enc_weight, enc_bias, dec_weight, dec_bias):
    loss_scale = 1.0 / math.sqrt(TOKENS)
    keep_mask = (token_ids != BEGIN_TOKEN).astype(jnp.float32)
    preact = jnp.zeros((TOKENS, LATENTS), jnp.float32) + enc_bias[None, :]
    for layer_index in range(LAYERS):
        preact = preact + jnp.dot(taps[layer_index], enc_weight[layer_index], preferred_element_type=jnp.float32)
    features = smooth_relu(preact).astype(jnp.bfloat16)
    colnorm = jnp.sqrt(lax.optimization_barrier(jnp.sum(jnp.square(dec_weight.astype(jnp.float32)), axis=1)) + 1e-06)
    feat_grads = loss_scale * SPARSITY * keep_mask[:, None] * lax.optimization_barrier(jnp.sum(colnorm, axis=0))[None, :]
    residues = []
    for layer_index in range(LAYERS):
        rebuilt = lax.dot_general(features, dec_weight[layer_index], (((1,), (1,)), ((), ())), preferred_element_type=jnp.float32)
        rebuilt = rebuilt + dec_bias[layer_index][None, :]
        residue = (loss_scale * keep_mask[:, None] * (rebuilt - taps[layer_index].astype(jnp.float32))).astype(jnp.bfloat16)
        residues.append(residue)
        feat_grads = feat_grads + jnp.dot(residue, dec_weight[layer_index], preferred_element_type=jnp.float32)
    pre_grads = (feat_grads * relu_slope(preact)).astype(jnp.bfloat16)
    enc_grads = []
    dec_grads = []
    for layer_index in range(LAYERS):
        enc_total = jnp.zeros((D, LATENTS), jnp.float32)
        dec_total = jnp.zeros((D, LATENTS), jnp.float32)
        normed = dec_weight[layer_index].astype(jnp.float32) / colnorm[layer_index][None, :]
        for block_index in range(N_TOKEN):
            first_row = block_index * TOK_DEV
            tap_block = taps[layer_index, first_row:first_row + TOK_DEV]
            grad_block = pre_grads[first_row:first_row + TOK_DEV]
            feat_block = features[first_row:first_row + TOK_DEV]
            residue_block = residues[layer_index][first_row:first_row + TOK_DEV]
            mask_block = keep_mask[first_row:first_row + TOK_DEV]
            enc_term = lax.dot_general(tap_block, grad_block, (((0,), (0,)), ((), ())), preferred_element_type=jnp.float32)
            enc_total = enc_total + lax.optimization_barrier(enc_term.astype(jnp.bfloat16)).astype(jnp.float32)
            activity = lax.optimization_barrier(jnp.sum(mask_block[:, None] * feat_block.astype(jnp.float32), axis=0))
            dec_term = lax.dot_general(residue_block, feat_block, (((0,), (0,)), ((), ())), preferred_element_type=jnp.float32)
            dec_term = dec_term + loss_scale * SPARSITY * activity[None, :] * normed
            dec_total = dec_total + lax.optimization_barrier(dec_term.astype(jnp.bfloat16)).astype(jnp.float32)
        enc_grads.append(enc_total.astype(jnp.bfloat16))
        dec_grads.append(dec_total.astype(jnp.bfloat16))
    return (jnp.stack(enc_grads), jnp.stack(dec_grads))
```

```python
import math

import jax
import jax.numpy as jnp
from jax import lax
from jax.sharding import PartitionSpec as P

KNEE_WIDTH = 0.5
SPARSITY = 0.5
BEGIN_TOKEN = 2
BF = jnp.bfloat16
F32 = jnp.float32


def smooth_relu(preact):
    positive = jnp.maximum(preact, 0.0)
    return jnp.where(
        positive < KNEE_WIDTH, positive * positive / (2.0 * KNEE_WIDTH), positive - 0.5 * KNEE_WIDTH
    )


def relu_slope(preact):
    return jnp.clip(preact / KNEE_WIDTH, 0.0, 1.0)


def general(taps, token_ids, enc_weight, enc_bias, dec_weight, dec_bias):
    tap_rows = taps[0]
    tokens_dev = tap_rows.shape[0]
    latent_dev = enc_weight.shape[2]
    row_block = enc_weight.shape[1]
    loss_scale = 1.0 / math.sqrt(tokens_dev * lax.axis_size("token"))
    keep_mask = (token_ids != BEGIN_TOKEN).astype(jnp.float32)
    spread = lax.all_to_all(tap_rows, "token", split_axis=1, concat_axis=0, tiled=True)
    partial_pre = lax.psum_scatter(
        jnp.dot(spread, enc_weight[0], preferred_element_type=jnp.float32),
        "token",
        scatter_dimension=0,
        tiled=True,
    )
    preact = lax.psum(partial_pre, "layer") + enc_bias[None, :]
    features = smooth_relu(preact).astype(jnp.bfloat16)
    dec_full = lax.all_gather(dec_weight[0], "token", axis=0, tiled=True)
    rebuilt_part = lax.dot_general(
        features, dec_full, (((1,), (1,)), ((), ())), preferred_element_type=jnp.float32
    )
    rebuilt = lax.psum(rebuilt_part, "latent") + dec_bias[0][None, :]
    residue = (loss_scale * keep_mask[:, None] * (rebuilt - tap_rows.astype(jnp.float32))).astype(
        jnp.bfloat16
    )
    colnorm = jnp.sqrt(jnp.sum(jnp.square(dec_full.astype(jnp.float32)), axis=0) + 1e-06)
    back_part = jnp.dot(residue, dec_full, preferred_element_type=jnp.float32)
    feat_back, norm_total = lax.psum((back_part, colnorm), "layer")
    feat_grads = feat_back + loss_scale * SPARSITY * keep_mask[:, None] * norm_total[None, :]
    pre_grads = (feat_grads * relu_slope(preact)).astype(jnp.bfloat16)
    activity = jnp.sum(keep_mask[:, None] * features.astype(jnp.float32), axis=0)
    penalty_scale = loss_scale * SPARSITY * activity / colnorm
    product = lax.dot_general(
        residue, features, (((0,), (0,)), ((), ())), preferred_element_type=jnp.float32
    )
    dec_grad = lax.psum_scatter(
        (product + dec_full.astype(jnp.float32) * penalty_scale[None, :]).astype(jnp.bfloat16),
        "token",
        scatter_dimension=0,
        tiled=True,
    )
    code_rows = lax.all_gather(pre_grads, "token", axis=0, tiled=True)
    blocks = lax.axis_size("token")
    spread_blocks = spread.reshape(blocks, tokens_dev, row_block)
    code_blocks = code_rows.reshape(blocks, tokens_dev, latent_dev)
    block_terms = jnp.einsum(
        "btd,btk->bdk", spread_blocks, code_blocks, preferred_element_type=jnp.float32
    )
    enc_grad = jnp.sum(
        lax.optimization_barrier(block_terms.astype(jnp.bfloat16)).astype(jnp.float32), axis=0
    )
    return (enc_grad.astype(jnp.bfloat16)[None], dec_grad[None])


def flip(x, axis, bit):
    n = lax.axis_size(axis)
    return lax.ppermute(x, axis, [(i, i ^ bit) for i in range(n)])


def swap_core(x):
    return flip(x, "layer", 1)


def swap_tok(x):
    return flip(x, "token", 1)


def swap_both(x):
    return lax.ppermute(x, ("layer", "token"), [(i, i ^ 3) for i in range(4)])


def dot(a, b):
    return jnp.dot(a, b, preferred_element_type=F32)


def dot_t(a, b):
    return lax.dot_general(a, b, (((1,), (1,)), ((), ())), preferred_element_type=F32)


def dot_rows(a, b):
    return lax.dot_general(a, b, (((0,), (0,)), ((), ())), preferred_element_type=F32)


def pick(flag, first, second):
    return jnp.where(flag == 0, first, second)


def folded(taps, token_ids, enc_weight, enc_bias, dec_weight, dec_bias):
    taps, enc_w, dec_w = taps[0], enc_weight[0], dec_weight[0]
    block, width = taps.shape
    half_d = enc_w.shape[0]
    quarter_d = half_d // 2
    half_t = block // 2
    sub_t = half_t // 2
    scale = 1.0 / math.sqrt(block * lax.axis_size("token"))
    tok, core, lat = (lax.axis_index(a) for a in ("token", "layer", "latent"))
    xb, nb, fb = lat & 1, (lat >> 1) & 1, (lat >> 2) & 1
    swap_x = lambda v: flip(v, "latent", 1)
    swap_n = lambda v: flip(v, "latent", 2)
    swap_f = lambda v: flip(v, "latent", 4)

    def rows(which_core, which_half):
        at = which_core * half_t
        parts = [
            lax.dynamic_slice(taps, (at + s * sub_t, which_half * half_d), (sub_t, half_d))
            for s in (nb, 1 - nb)
        ]
        return jnp.concatenate(parts, 0)

    t_diag = swap_both(rows(1 - core, 1 - tok))
    t_same = swap_tok(rows(core, 1 - tok))
    enc_o = swap_core(enc_w)
    own_mine = rows(core, tok)
    own_rest = rows(1 - core, tok)
    t_core = swap_core(own_rest)
    dec_o = swap_core(dec_w)
    rest_same = swap_core(t_diag)

    keep_all = (token_ids != BEGIN_TOKEN).astype(F32)
    keep_far = swap_tok(keep_all)

    def keep_rows(v):
        return jnp.concatenate(
            [lax.dynamic_slice(v, (core * half_t + s * sub_t,), (sub_t,)) for s in (nb, 1 - nb)], 0
        )

    keep_own, keep_oth = keep_rows(keep_all), keep_rows(keep_far)
    keep = jnp.concatenate([pick(xb, keep_own, keep_oth), pick(xb, keep_oth, keep_own)], 0)

    sq = jnp.sum(jnp.square(dec_w.astype(F32)), axis=0)
    colnorm = jnp.sqrt(sq + swap_tok(sq) + 1e-06)
    norm_total = colnorm + swap_core(colnorm)
    bias_o = swap_core(dec_bias)

    pre_own = dot(own_mine, enc_w) + dot(t_core, enc_o)
    far_oth = swap_tok(pre_own.astype(BF))
    pre_oth = dot(t_same, enc_w) + dot(t_diag, enc_o)
    far_own = swap_tok(pre_oth.astype(BF))
    pre_own = pre_own + far_own.astype(F32)
    pre_oth = pre_oth + far_oth.astype(F32)
    preact = jnp.concatenate([pick(xb, pre_own, pre_oth), pick(xb, pre_oth, pre_own)], 0)
    preact = preact + enc_bias[None, :]
    feats = smooth_relu(preact).astype(BF)
    feats_o = swap_core(feats)

    group = lambda v, g: v[g * sub_t : (g + 1) * sub_t]
    f = [group(feats, g) for g in range(4)]
    a3 = swap_x(dot_t(f[3], dec_w).astype(BF))
    b3 = swap_n(dot_t(f[3], dec_o).astype(BF))
    a1 = swap_n((dot_t(f[1], dec_w) + a3.astype(F32)).astype(BF))
    a2 = swap_x(dot_t(f[2], dec_w).astype(BF))
    b2 = swap_x((dot_t(f[2], dec_o) + b3.astype(F32)).astype(BF))
    b1 = swap_n(dot_t(f[1], dec_o).astype(BF))

    keep0 = keep[:sub_t]
    tap_a = pick(xb, own_mine[:sub_t], t_same[:sub_t])
    tap_b = pick(xb, t_core[:sub_t], t_diag[:sub_t])

    def shard(v, at):
        return lax.dynamic_slice_in_dim(v, at * quarter_d, quarter_d, 1)

    def finish(sum0, tap, bias):
        far = swap_f(shard(sum0, 1 - fb).astype(BF))
        rebuilt = shard(sum0, fb) + far.astype(F32)
        bias = lax.dynamic_slice(bias[0], (tok * half_d + fb * quarter_d,), (quarter_d,))
        res = scale * keep0[:, None] * (rebuilt + bias[None, :] - shard(tap, fb).astype(F32))
        res = res.astype(BF)
        far = swap_f(res)
        return jnp.concatenate([pick(fb, res, far), pick(fb, far, res)], 1)

    ra0 = finish(dot_t(f[0], dec_w) + a1.astype(F32) + a2.astype(F32), tap_a, dec_bias)
    ra1, ra2 = swap_n(ra0), swap_x(ra0)
    rb0 = finish(dot_t(f[0], dec_o) + b1.astype(F32) + b2.astype(F32), tap_b, bias_o)
    rb1, rb2 = swap_n(rb0), swap_x(rb0)
    ra3 = swap_x(ra1)
    rb3 = swap_n(rb2)
    res_a = jnp.concatenate([ra0, ra1, ra2, ra3], 0)
    res_b = jnp.concatenate([rb0, rb1, rb2, rb3], 0)
    res_o = swap_core(res_b)

    back = dot(res_a, dec_w) + dot(res_b, dec_o)
    back_far = swap_tok(back.astype(BF))
    back_far = jnp.concatenate([back_far[half_t:], back_far[:half_t]], 0).astype(F32)
    fg = back + back_far + scale * SPARSITY * keep[:, None] * norm_total[None, :]
    pre_g = (fg * relu_slope(preact)).astype(BF)
    pre_g_o = swap_core(pre_g)

    both_keep = swap_core(keep)
    activity = jnp.sum(keep[:, None] * feats.astype(F32), axis=0) + jnp.sum(
        both_keep[:, None] * feats_o.astype(F32), axis=0
    )
    penalty = scale * SPARSITY * activity / colnorm
    prod = dot_rows(
        jnp.concatenate([res_a, res_o], 0), jnp.concatenate([feats, feats_o], 0)
    )
    dec_grad = (prod + dec_w.astype(F32) * penalty[None, :]).astype(BF)

    def ordered(own, oth):
        return jnp.concatenate([pick(xb, own, oth), pick(xb, oth, own)], 0)

    tap_rows = jnp.concatenate([ordered(own_mine, t_same), ordered(own_rest, rest_same)], 0)
    enc_grad = dot_rows(tap_rows, jnp.concatenate([pre_g, pre_g_o], 0)).astype(BF)
    return (enc_grad[None], dec_grad[None])


def solution(mesh):
    placed = (
        P("layer", "token", None),
        P("token"),
        P("layer", "token", "latent"),
        P("latent"),
        P("layer", "token", "latent"),
        P("layer", None),
    )
    shape = dict(mesh.shape)
    foldable = shape["layer"] == 2 and shape["token"] == 2 and shape["latent"] == 8
    return jax.shard_map(
        folded if foldable else general,
        mesh=mesh,
        in_specs=placed,
        out_specs=(P("layer", "token", "latent"), P("layer", "token", "latent")),
        check_vma=False,
    )
```

```python
import math

import jax
import jax.numpy as jnp
from jax import lax
from jax.sharding import PartitionSpec as P


KNEE_WIDTH = 0.5
SPARSITY = 0.5
BEGIN_TOKEN = 2
BF = jnp.bfloat16
F32 = jnp.float32


def smooth_relu(preact):
    positive = jnp.maximum(preact, 0.0)
    return jnp.where(
        positive < KNEE_WIDTH, positive * positive / (2.0 * KNEE_WIDTH), positive - 0.5 * KNEE_WIDTH
    )


def relu_slope(preact):
    return jnp.clip(preact / KNEE_WIDTH, 0.0, 1.0)


def general(taps, token_ids, enc_weight, enc_bias, dec_weight, dec_bias):
    tap_rows = taps[0]
    tokens_dev = tap_rows.shape[0]
    latent_dev = enc_weight.shape[2]
    row_block = enc_weight.shape[1]
    loss_scale = 1.0 / math.sqrt(tokens_dev * lax.axis_size("token"))
    keep_mask = (token_ids != BEGIN_TOKEN).astype(jnp.float32)
    spread = lax.all_to_all(tap_rows, "token", split_axis=1, concat_axis=0, tiled=True)
    partial_pre = lax.psum_scatter(
        jnp.dot(spread, enc_weight[0], preferred_element_type=jnp.float32),
        "token",
        scatter_dimension=0,
        tiled=True,
    )
    preact = lax.psum(partial_pre, "layer") + enc_bias[None, :]
    features = smooth_relu(preact).astype(jnp.bfloat16)
    dec_full = lax.all_gather(dec_weight[0], "token", axis=0, tiled=True)
    rebuilt_part = lax.dot_general(
        features, dec_full, (((1,), (1,)), ((), ())), preferred_element_type=jnp.float32
    )
    rebuilt = lax.psum(rebuilt_part, "latent") + dec_bias[0][None, :]
    residue = (loss_scale * keep_mask[:, None] * (rebuilt - tap_rows.astype(jnp.float32))).astype(
        jnp.bfloat16
    )
    colnorm = jnp.sqrt(jnp.sum(jnp.square(dec_full.astype(jnp.float32)), axis=0) + 1e-06)
    back_part = jnp.dot(residue, dec_full, preferred_element_type=jnp.float32)
    feat_back, norm_total = lax.psum((back_part, colnorm), "layer")
    feat_grads = feat_back + loss_scale * SPARSITY * keep_mask[:, None] * norm_total[None, :]
    pre_grads = (feat_grads * relu_slope(preact)).astype(jnp.bfloat16)
    activity = jnp.sum(keep_mask[:, None] * features.astype(jnp.float32), axis=0)
    penalty_scale = loss_scale * SPARSITY * activity / colnorm
    product = lax.dot_general(
        residue, features, (((0,), (0,)), ((), ())), preferred_element_type=jnp.float32
    )
    dec_grad = lax.psum_scatter(
        (product + dec_full.astype(jnp.float32) * penalty_scale[None, :]).astype(jnp.bfloat16),
        "token",
        scatter_dimension=0,
        tiled=True,
    )
    code_rows = lax.all_gather(pre_grads, "token", axis=0, tiled=True)
    blocks = lax.axis_size("token")
    spread_blocks = spread.reshape(blocks, tokens_dev, row_block)
    code_blocks = code_rows.reshape(blocks, tokens_dev, latent_dev)
    block_terms = jnp.einsum(
        "btd,btk->bdk", spread_blocks, code_blocks, preferred_element_type=jnp.float32
    )
    enc_grad = jnp.sum(
        lax.optimization_barrier(block_terms.astype(jnp.bfloat16)).astype(jnp.float32), axis=0
    )
    return (enc_grad.astype(jnp.bfloat16)[None], dec_grad[None])


def flip(x, axis, bit):
    n = lax.axis_size(axis)
    return lax.ppermute(x, axis, [(i, i ^ bit) for i in range(n)])


def swap_core(x):
    return flip(x, "layer", 1)


def swap_tok(x):
    return flip(x, "token", 1)


def swap_both(x):
    return lax.ppermute(x, ("layer", "token"), [(i, i ^ 3) for i in range(4)])


def dot(a, b):
    return jnp.dot(a, b, preferred_element_type=F32)


def dot_t(a, b):
    return lax.dot_general(a, b, (((1,), (1,)), ((), ())), preferred_element_type=F32)


def dot_rows(a, b):
    return lax.dot_general(a, b, (((0,), (0,)), ((), ())), preferred_element_type=F32)


def pick(flag, first, second):
    return jnp.where(flag == 0, first, second)


def folded(taps, token_ids, enc_weight, enc_bias, dec_weight, dec_bias):
    return folded_body(taps, token_ids, enc_weight, enc_bias, dec_weight, dec_bias)


def folded_body(taps, token_ids, enc_weight, enc_bias, dec_weight, dec_bias):
    taps, enc_w, dec_w = taps[0], enc_weight[0], dec_weight[0]
    block, _ = taps.shape
    half_d = enc_w.shape[0]
    quarter_d = half_d // 2
    half_t = block // 2
    sub_t = half_t // 2
    scale = 1.0 / math.sqrt(block * lax.axis_size("token"))
    tok, core, lat = (lax.axis_index(a) for a in ("token", "layer", "latent"))
    xb, nb, fb = lat & 1, (lat >> 1) & 1, (lat >> 2) & 1
    swap_x = lambda v: flip(v, "latent", 1)
    swap_n = lambda v: flip(v, "latent", 2)
    swap_f = lambda v: flip(v, "latent", 4)
    sub_at = (nb, 1 - nb)

    def sub_rows(which_core, sub, which_half):
        at = which_core * half_t + sub_at[sub] * sub_t
        return lax.dynamic_slice(taps, (at, which_half * half_d), (sub_t, half_d))

    def core_rows(which_core):
        return lax.dynamic_slice(taps, (which_core * half_t, tok * half_d), (half_t, half_d))

    def after(v):
        nonlocal taps
        taps, v = lax.optimization_barrier((taps, v))
        return v

    d1 = swap_both(after(sub_rows(1 - core, 1, 1 - tok)))
    s1 = swap_tok(after(sub_rows(core, 1, 1 - tok)))
    enc_o = swap_core(enc_w)
    own_rest = after(core_rows(1 - core))
    t_core = swap_core(own_rest)
    own_mine = after(core_rows(core))
    d0 = swap_both(after(sub_rows(1 - core, 0, 1 - tok)))
    s0 = swap_tok(after(sub_rows(core, 0, 1 - tok)))
    dec_o = swap_core(dec_w)
    bias_o = swap_core(dec_bias)

    def by_sub(v):
        halves = v[:sub_t], v[sub_t:]
        return pick(nb, *halves), pick(nb, halves[1], halves[0])

    pre_own = dot(own_mine, enc_w) + dot(t_core, enc_o)
    far_oth = by_sub(swap_tok(pre_own.astype(BF)).astype(F32))
    pre_own = by_sub(pre_own)

    def activate(s, same, diag, earlier=None):
        pre_oth = dot(same, enc_w) + dot(diag, enc_o)
        far = swap_tok(pre_oth.astype(BF))
        if earlier is not None:
            far, _ = lax.optimization_barrier((far, earlier))
        own = pre_own[s] + far.astype(F32)
        oth = pre_oth + far_oth[s]
        pre = [pick(xb, own, oth) + enc_bias[None, :], pick(xb, oth, own) + enc_bias[None, :]]
        return pre, [smooth_relu(p).astype(BF) for p in pre]

    (p1, p3), (f1, f3) = activate(1, s1, d1)
    a3 = swap_x(dot_t(f3, dec_w).astype(BF))
    b3 = swap_n(dot_t(f3, dec_o).astype(BF))
    b1 = swap_n(dot_t(f1, dec_o).astype(BF))
    a1 = swap_n((dot_t(f1, dec_w) + a3.astype(F32)).astype(BF))
    (p0, p2), (f0, f2) = activate(0, s0, d0, f3)
    a2 = swap_x(dot_t(f2, dec_w).astype(BF))
    b2 = swap_x((dot_t(f2, dec_o) + b3.astype(F32)).astype(BF))
    preact = jnp.concatenate([p0, p1, p2, p3], 0)
    feats = jnp.concatenate(lax.optimization_barrier((f0, f1, f2, f3)), 0)

    keep_all = (token_ids != BEGIN_TOKEN).astype(F32)
    sq = jnp.sum(jnp.square(dec_w.astype(F32)), axis=0)
    small = jnp.concatenate([keep_all, sq])
    small_far = swap_tok(small)
    keep_far = small_far[:block]
    colnorm = jnp.sqrt(sq + small_far[block:] + 1e-06)
    norm_total = colnorm + swap_core(colnorm)
    keep_sub = lambda v, s: lax.dynamic_slice(v, (core * half_t + sub_at[s] * sub_t,), (sub_t,))
    keeps = [[keep_sub(v, s) for s in (0, 1)] for v in (keep_all, keep_far)]
    keep = jnp.concatenate(
        [pick(xb, keeps[0][s], keeps[1][s]) for s in (0, 1)]
        + [pick(xb, keeps[1][s], keeps[0][s]) for s in (0, 1)]
    )
    tap_at = lambda v: lax.dynamic_slice(v, (nb * sub_t, fb * quarter_d), (sub_t, quarter_d))

    def shard(v, at):
        return lax.dynamic_slice_in_dim(v, at * quarter_d, quarter_d, 1)

    keep0 = keep[:sub_t]
    tap_a = pick(xb, tap_at(own_mine), shard(s0, fb))
    tap_b = pick(xb, tap_at(t_core), shard(d0, fb))

    def finish(sum0, tap, bias, earlier=None):
        far = swap_f(shard(sum0, 1 - fb).astype(BF))
        if earlier is not None:
            far, _ = lax.optimization_barrier((far, earlier))
        rebuilt = shard(sum0, fb) + far.astype(F32)
        bias = lax.dynamic_slice(bias[0], (tok * half_d + fb * quarter_d,), (quarter_d,))
        res = scale * keep0[:, None] * (rebuilt + bias[None, :] - tap.astype(F32))
        res = res.astype(BF)
        far = swap_f(res)
        return res, jnp.concatenate([pick(fb, res, far), pick(fb, far, res)], 1)

    res, ra0 = finish(dot_t(f0, dec_w) + a1.astype(F32) + a2.astype(F32), tap_a, dec_bias)
    _, rb0 = finish(dot_t(f0, dec_o) + b1.astype(F32) + b2.astype(F32), tap_b, bias_o, res)
    ra2, ra1 = swap_x(ra0), swap_n(ra0)
    rb2, rb1 = swap_x(rb0), swap_n(rb0)
    ra3 = swap_x(ra1)
    rb3 = swap_n(rb2)
    res_a = jnp.concatenate([ra0, ra1, ra2, ra3], 0)
    res_b = jnp.concatenate([rb0, rb1, rb2, rb3], 0)
    res_o = swap_core(res_b)

    back = dot(res_a, dec_w) + dot(res_b, dec_o)
    back_far = swap_tok(back.astype(BF))
    back_far = jnp.concatenate([back_far[half_t:], back_far[:half_t]], 0).astype(F32)
    fg = back + back_far + scale * SPARSITY * keep[:, None] * norm_total[None, :]
    pre_g = (fg * relu_slope(preact)).astype(BF)

    feats_o = swap_core(feats)
    active = swap_core(jnp.sum(keep[:, None] * feats.astype(F32), axis=0))
    activity = jnp.sum(keep[:, None] * feats.astype(F32), axis=0) + active
    penalty = scale * SPARSITY * activity / colnorm
    prod = dot_rows(jnp.concatenate([res_a, res_o], 0), jnp.concatenate([feats, feats_o], 0))
    dec_grad = (prod + dec_w.astype(F32) * penalty[None, :]).astype(BF)

    pg = [pre_g[g * sub_t : (g + 1) * sub_t] for g in range(4)]
    pg_own = [pick(xb, pg[0], pg[2]), pick(xb, pg[1], pg[3])]
    pg_oth = [pick(xb, pg[2], pg[0]), pick(xb, pg[3], pg[1])]
    pg_own = [pick(nb, *pg_own), pick(nb, pg_own[1], pg_own[0])]
    pg = jnp.concatenate(pg_own + pg_oth, 0)
    pg_o = swap_core(pg)
    rest0, rest1 = swap_core(d0), swap_core(d1)
    tap_rows = jnp.concatenate([own_mine, s0, s1, own_rest, rest0, rest1], 0)
    enc_grad = dot_rows(tap_rows, jnp.concatenate([pg, pg_o], 0)).astype(BF)
    return (enc_grad[None], dec_grad[None])


def solution(mesh):
    placed = (
        P("layer", "token", None),
        P("token"),
        P("layer", "token", "latent"),
        P("latent"),
        P("layer", "token", "latent"),
        P("layer", None),
    )
    shape = dict(mesh.shape)
    foldable = shape["layer"] == 2 and shape["token"] == 2 and shape["latent"] == 8
    return jax.shard_map(
        folded if foldable else general,
        mesh=mesh,
        in_specs=placed,
        out_specs=(P("layer", "token", "latent"), P("layer", "token", "latent")),
        check_vma=False,
    )
```

```python
import math

import jax
import jax.numpy as jnp
from jax import lax
from jax.sharding import PartitionSpec as P


KNEE_WIDTH = 0.5
SPARSITY = 0.5
BEGIN_TOKEN = 2
BF = jnp.bfloat16
F32 = jnp.float32


def smooth_relu(preact):
    positive = jnp.maximum(preact, 0.0)
    return jnp.where(
        positive < KNEE_WIDTH, positive * positive / (2.0 * KNEE_WIDTH), positive - 0.5 * KNEE_WIDTH
    )


def relu_slope(preact):
    return jnp.clip(preact / KNEE_WIDTH, 0.0, 1.0)


def general(taps, token_ids, enc_weight, enc_bias, dec_weight, dec_bias):
    tap_rows = taps[0]
    tokens_dev = tap_rows.shape[0]
    latent_dev = enc_weight.shape[2]
    row_block = enc_weight.shape[1]
    loss_scale = 1.0 / math.sqrt(tokens_dev * lax.axis_size("token"))
    keep_mask = (token_ids != BEGIN_TOKEN).astype(jnp.float32)
    spread = lax.all_to_all(tap_rows, "token", split_axis=1, concat_axis=0, tiled=True)
    partial_pre = lax.psum_scatter(
        jnp.dot(spread, enc_weight[0], preferred_element_type=jnp.float32),
        "token",
        scatter_dimension=0,
        tiled=True,
    )
    preact = lax.psum(partial_pre, "layer") + enc_bias[None, :]
    features = smooth_relu(preact).astype(jnp.bfloat16)
    dec_full = lax.all_gather(dec_weight[0], "token", axis=0, tiled=True)
    rebuilt_part = lax.dot_general(
        features, dec_full, (((1,), (1,)), ((), ())), preferred_element_type=jnp.float32
    )
    rebuilt = lax.psum(rebuilt_part, "latent") + dec_bias[0][None, :]
    residue = (loss_scale * keep_mask[:, None] * (rebuilt - tap_rows.astype(jnp.float32))).astype(
        jnp.bfloat16
    )
    colnorm = jnp.sqrt(jnp.sum(jnp.square(dec_full.astype(jnp.float32)), axis=0) + 1e-06)
    back_part = jnp.dot(residue, dec_full, preferred_element_type=jnp.float32)
    feat_back, norm_total = lax.psum((back_part, colnorm), "layer")
    feat_grads = feat_back + loss_scale * SPARSITY * keep_mask[:, None] * norm_total[None, :]
    pre_grads = (feat_grads * relu_slope(preact)).astype(jnp.bfloat16)
    activity = jnp.sum(keep_mask[:, None] * features.astype(jnp.float32), axis=0)
    penalty_scale = loss_scale * SPARSITY * activity / colnorm
    product = lax.dot_general(
        residue, features, (((0,), (0,)), ((), ())), preferred_element_type=jnp.float32
    )
    dec_grad = lax.psum_scatter(
        (product + dec_full.astype(jnp.float32) * penalty_scale[None, :]).astype(jnp.bfloat16),
        "token",
        scatter_dimension=0,
        tiled=True,
    )
    code_rows = lax.all_gather(pre_grads, "token", axis=0, tiled=True)
    blocks = lax.axis_size("token")
    spread_blocks = spread.reshape(blocks, tokens_dev, row_block)
    code_blocks = code_rows.reshape(blocks, tokens_dev, latent_dev)
    block_terms = jnp.einsum(
        "btd,btk->bdk", spread_blocks, code_blocks, preferred_element_type=jnp.float32
    )
    enc_grad = jnp.sum(
        lax.optimization_barrier(block_terms.astype(jnp.bfloat16)).astype(jnp.float32), axis=0
    )
    return (enc_grad.astype(jnp.bfloat16)[None], dec_grad[None])


def flip(x, axis, bit):
    n = lax.axis_size(axis)
    return lax.ppermute(x, axis, [(i, i ^ bit) for i in range(n)])


def swap_core(x):
    return flip(x, "layer", 1)


def swap_tok(x):
    return flip(x, "token", 1)


def swap_both(x):
    return lax.ppermute(x, ("layer", "token"), [(i, i ^ 3) for i in range(4)])


def dot(a, b):
    return jnp.dot(a, b, preferred_element_type=F32)


def dot_t(a, b):
    return lax.dot_general(a, b, (((1,), (1,)), ((), ())), preferred_element_type=F32)


def dot_rows(a, b):
    return lax.dot_general(a, b, (((0,), (0,)), ((), ())), preferred_element_type=F32)


def pick(flag, first, second):
    return jnp.where(flag == 0, first, second)


def folded(taps, token_ids, enc_weight, enc_bias, dec_weight, dec_bias):
    return folded_body(taps, token_ids, enc_weight, enc_bias, dec_weight, dec_bias)


def folded_body(taps, token_ids, enc_weight, enc_bias, dec_weight, dec_bias):
    taps, enc_w, dec_w = taps[0], enc_weight[0], dec_weight[0]
    block, _ = taps.shape
    half_d = enc_w.shape[0]
    quarter_d = half_d // 2
    half_t = block // 2
    sub_t = half_t // 2
    scale = 1.0 / math.sqrt(block * lax.axis_size("token"))
    tok, core, lat = (lax.axis_index(a) for a in ("token", "layer", "latent"))
    xb, nb, fb = lat & 1, (lat >> 1) & 1, (lat >> 2) & 1
    swap_x = lambda v: flip(v, "latent", 1)
    swap_n = lambda v: flip(v, "latent", 2)
    swap_f = lambda v: flip(v, "latent", 4)
    sub_at = (nb, 1 - nb)

    def sub_rows(which_core, sub, which_half):
        at = which_core * half_t + sub_at[sub] * sub_t
        return lax.dynamic_slice(taps, (at, which_half * half_d), (sub_t, half_d))

    def core_rows(which_core):
        return lax.dynamic_slice(taps, (which_core * half_t, tok * half_d), (half_t, half_d))

    sent = (sub_rows(1 - core, 1, 1 - tok), sub_rows(core, 1, 1 - tok)) + (
        sub_rows(1 - core, 0, 1 - tok), sub_rows(core, 0, 1 - tok)
    )
    taps, *sent = lax.optimization_barrier((taps, *sent))
    d1, s1 = swap_both(sent[0]), swap_tok(sent[1])
    enc_o = swap_core(enc_w)
    own_rest, own_mine = core_rows(1 - core), core_rows(core)
    t_core = swap_core(own_rest)
    d0, s0 = swap_both(sent[2]), swap_tok(sent[3])
    dec_o = swap_core(dec_w)
    bias_o = swap_core(dec_bias)

    def by_sub(v):
        halves = v[:sub_t], v[sub_t:]
        return pick(nb, *halves), pick(nb, halves[1], halves[0])

    enc_all = lax.optimization_barrier(jnp.concatenate([enc_w, enc_o], 0))

    def encode(own_layer, other_layer):
        return dot(own_layer, enc_all[:half_d]) + dot(other_layer, enc_all[half_d:])

    pre_own = encode(own_mine, t_core)
    far_oth = by_sub(swap_tok(pre_own.astype(BF)))
    pre_own = by_sub(pre_own)

    def activate(s, same, diag, earlier=None):
        pre_oth = encode(same, diag)
        far = swap_tok(pre_oth.astype(BF))
        if earlier is not None:
            far, _ = lax.optimization_barrier((far, earlier))
        own = pre_own[s] + far.astype(F32)
        oth = pre_oth + far_oth[s].astype(F32)
        pre = [pick(xb, own, oth) + enc_bias[None, :], pick(xb, oth, own) + enc_bias[None, :]]
        return pre, [smooth_relu(p).astype(BF) for p in pre]

    (p1, p3), (f1, f3) = activate(1, s1, d1)
    a3 = swap_x(dot_t(f3, dec_w).astype(BF))
    b3 = swap_n(dot_t(f3, dec_o).astype(BF))
    b1 = swap_n(dot_t(f1, dec_o).astype(BF))
    a1 = swap_n((dot_t(f1, dec_w) + a3.astype(F32)).astype(BF))
    (p0, p2), (f0, f2) = activate(0, s0, d0, f3)
    a2 = swap_x(dot_t(f2, dec_w).astype(BF))
    b2 = swap_x((dot_t(f2, dec_o) + b3.astype(F32)).astype(BF))

    token_ids, dec_late, dec_bias, bias_o, _ = lax.optimization_barrier(
        (token_ids, dec_w, dec_bias, bias_o, f2)
    )
    keep_all = (token_ids != BEGIN_TOKEN).astype(F32)
    sq = jnp.sum(jnp.square(dec_late.astype(F32)), axis=0)
    small = jnp.concatenate([keep_all, sq])
    small_far = swap_tok(small)
    keep_far = small_far[:block]
    keep_sub = lambda v, s: lax.dynamic_slice(v, (core * half_t + sub_at[s] * sub_t,), (sub_t,))
    keeps = [[keep_sub(v, s) for s in (0, 1)] for v in (keep_all, keep_far)]
    keep = jnp.concatenate(
        [pick(xb, keeps[0][s], keeps[1][s]) for s in (0, 1)]
        + [pick(xb, keeps[1][s], keeps[0][s]) for s in (0, 1)]
    )
    tap_at = lambda v: lax.dynamic_slice(v, (nb * sub_t, fb * quarter_d), (sub_t, quarter_d))

    def shard(v, at):
        return lax.dynamic_slice_in_dim(v, at * quarter_d, quarter_d, 1)

    keep0 = keep[:sub_t]
    tap_a = pick(xb, tap_at(own_mine), shard(s0, fb))
    tap_b = pick(xb, tap_at(t_core), shard(d0, fb))

    def finish(sum0, tap, bias, earlier=None):
        far = swap_f(shard(sum0, 1 - fb).astype(BF))
        if earlier is not None:
            far, _ = lax.optimization_barrier((far, earlier))
        rebuilt = shard(sum0, fb) + far.astype(F32)
        bias = lax.dynamic_slice(bias[0], (tok * half_d + fb * quarter_d,), (quarter_d,))
        res = scale * keep0[:, None] * (rebuilt + bias[None, :] - tap.astype(F32))
        res = res.astype(BF)
        far = swap_f(res)
        return res, jnp.concatenate([pick(fb, res, far), pick(fb, far, res)], 1)

    res, ra0 = finish(dot_t(f0, dec_w) + a1.astype(F32) + a2.astype(F32), tap_a, dec_bias)
    _, rb0 = finish(dot_t(f0, dec_o) + b1.astype(F32) + b2.astype(F32), tap_b, bias_o, res)

    own_mine, own_rest, s0, s1, d0, d1, f0, f1, f2, f3, _ = lax.optimization_barrier(
        (own_mine, own_rest, s0, s1, d0, d1, f0, f1, f2, f3, res)
    )
    preact = jnp.concatenate([p0, p1, p2, p3], 0)
    feats = jnp.concatenate([f0, f1, f2, f3], 0)
    colnorm = jnp.sqrt(sq + small_far[block:] + 1e-06)
    norm_total = colnorm + swap_core(colnorm)
    ra2, ra1 = swap_x(ra0), swap_n(ra0)
    rb2, rb1 = swap_x(rb0), swap_n(rb0)
    ra3 = swap_x(ra1)
    rb3 = swap_n(rb2)
    res_a = jnp.concatenate([ra0, ra1, ra2, ra3], 0)
    res_b = jnp.concatenate([rb0, rb1, rb2, rb3], 0)
    res_o = swap_core(res_b)

    back = dot(res_a, dec_w) + dot(res_b, dec_o)
    back_far = swap_tok(back.astype(BF))
    back_far = jnp.concatenate([back_far[half_t:], back_far[:half_t]], 0).astype(F32)
    fg = back + back_far + scale * SPARSITY * keep[:, None] * norm_total[None, :]
    pre_g = (fg * relu_slope(preact)).astype(BF)

    feats_o = swap_core(feats)
    active = swap_core(jnp.sum(keep[:, None] * feats.astype(F32), axis=0))
    activity = jnp.sum(keep[:, None] * feats.astype(F32), axis=0) + active
    penalty = scale * SPARSITY * activity / colnorm
    prod = dot_rows(jnp.concatenate([res_a, res_o], 0), jnp.concatenate([feats, feats_o], 0))
    dec_grad = (prod + dec_w.astype(F32) * penalty[None, :]).astype(BF)

    pg = [pre_g[g * sub_t : (g + 1) * sub_t] for g in range(4)]
    pg_own = [pick(xb, pg[0], pg[2]), pick(xb, pg[1], pg[3])]
    pg_oth = [pick(xb, pg[2], pg[0]), pick(xb, pg[3], pg[1])]
    pg_own = [pick(nb, *pg_own), pick(nb, pg_own[1], pg_own[0])]
    pg = jnp.concatenate(pg_own + pg_oth, 0)
    pg_o = swap_core(pg)
    rest0, rest1 = swap_core(d0), swap_core(d1)
    tap_rows = jnp.concatenate([own_mine, s0, s1, own_rest, rest0, rest1], 0)
    enc_grad = dot_rows(tap_rows, jnp.concatenate([pg, pg_o], 0)).astype(BF)
    return (enc_grad[None], dec_grad[None])


def solution(mesh):
    placed = (
        P("layer", "token", None),
        P("token"),
        P("layer", "token", "latent"),
        P("latent"),
        P("layer", "token", "latent"),
        P("layer", None),
    )
    shape = dict(mesh.shape)
    foldable = shape["layer"] == 2 and shape["token"] == 2 and shape["latent"] == 8
    return jax.shard_map(
        folded if foldable else general,
        mesh=mesh,
        in_specs=placed,
        out_specs=(P("layer", "token", "latent"), P("layer", "token", "latent")),
        check_vma=False,
    )
```
